1024 devices in a mesh: row: 16 (over z, core), col: 64 (over x, y).
Axes of the slice: x: 8, y: 8, z: 8, core: 2. Of those that a mesh axis runs over, the one named last changes fastest.
Arguments:
- matrix: float32 [12288, 24576], P('row', 'col'), may hold values from -6 to 6
- panel_t: float32 [512, 12288], P('col', 'row'), may hold values from -0.25 to 0.25
- inverse_lower: float32 [512, 512], replicated, as said below
- pivot_rows: int32 [512], replicated, may hold values from 0 to 12287, as said below
Outputs:
- updated: float32 [12288, 24576], P('row', 'col')
The draws below stay inside these ranges and needn't reach their ends.
Inputs may be any that keep to these rules, and one draw needn't show every extreme that they name: `pivot_rows`: entries are distinct; entry j is either j itself or a row at or past 768, so the interchanges are disjoint swaps. Exactly 256 entries differ from their position. The rows of one index of row are named by at most 32 entries, and in every draw some index of row is named by exactly 32. `inverse_lower`: zero above the diagonal and one on it.
All inputs are finite; a program needn't handle non-finite values.
Results may differ from the reference program's by a relative error of at most 0.000058.
Values sent between devices are 32-bit elements; how exact they have to be, the bound alone decides.
A program may use at most 32 MiB of HBM per device.

```python
import jax
import jax.numpy as jnp
from jax import lax

NB = 512
ROWS_DEV = 768
NR = 12288
NC = 24576
N_ROW = 16


def draw_inverse_lower(key, part):
    values = jax.random.normal(key, (NB, NB), jnp.float32) / NB ** 0.5
    return jnp.tril(values, -1) + jnp.eye(NB, dtype=jnp.float32)


def draw_pivot_rows(key, part):
    slot_count = NB // N_ROW
    other_count = N_ROW - 1
    first_key, second_key, third_key, fourth_key = jax.random.split(key, 4)
    device_keys = jax.random.split(first_key, other_count)
    offsets = jax.vmap(lambda k: jax.random.permutation(k, ROWS_DEV)[:slot_count])(device_keys).astype(jnp.int32)
    fullest = jax.random.randint(second_key, (), 0, other_count).astype(jnp.int32)
    order = (fullest + jnp.arange(other_count, dtype=jnp.int32)) % other_count
    devices = 1 + order
    candidates = devices[:, None] * ROWS_DEV + jnp.take(offsets, order, axis=0)
    leading = candidates[0]
    others = jax.random.permutation(third_key, candidates[1:].reshape(-1)).astype(jnp.int32)
    pool = jnp.concatenate([leading, others]).astype(jnp.int32)
    column_order = jax.random.permutation(fourth_key, NB).astype(jnp.int32)
    rank = jnp.zeros((NB,), jnp.int32).at[column_order].set(jnp.arange(NB, dtype=jnp.int32))
    half = NB // 2
    moved = rank < half
    chosen = jnp.take(pool, jnp.clip(rank, 0, half - 1), axis=0)
    places = jnp.arange(NB, dtype=jnp.int32)
    return jnp.where(moved, chosen, places).astype(jnp.int32)


def levels(key, shape, cuts, least, high):
    def one(dim, blocks):
        steps = jax.random.uniform(jax.random.fold_in(jax.random.fold_in(key, 6), dim), (blocks,), jnp.float32, least / len(cuts), high / len(cuts))
        return jnp.repeat(jnp.exp(steps), shape[dim] // blocks).reshape((-1,) + (1,) * (len(shape) - dim - 1))

    level = one(*cuts[0])
    for cut in cuts[1:]:
        level = level * one(*cut)
    return level


def bell_draw(stream_key, extent, scale, reach, cuts=(), kind=jnp.bfloat16):
    entries = jax.random.normal(stream_key, extent, jnp.float32) * scale
    if len(cuts) > 0:
        entries = levels(stream_key, extent, cuts, -0.22, 0.18) * entries
    return jnp.clip(entries, min=-reach, max=reach).astype(kind)


def setup_inputs(seed: int = 0) -> dict:
    arg_keys = jax.random.split(jax.random.key(seed), 5)
    matrix = bell_draw(arg_keys[0], (NR, NC), 1.0, 6.0, ((0, 16), (1, 64)), jnp.float32)
    panel_t = bell_draw(arg_keys[1], (NB, NR), NB ** -0.5, 0.25, ((0, 64), (1, 16)), jnp.float32)
    inverse_lower = draw_inverse_lower(jax.random.fold_in(arg_keys[4], 71), 0)
    pivot_rows = draw_pivot_rows(jax.random.fold_in(arg_keys[4], 71), 0)
    return dict(matrix=matrix, panel_t=panel_t, inverse_lower=inverse_lower, pivot_rows=pivot_rows)


def reference(matrix, panel_t, inverse_lower, pivot_rows):
    total_rows = matrix.shape[0]
    width = inverse_lower.shape[0]
    places = jnp.arange(width, dtype=jnp.int32)
    moved = pivot_rows != places
    picked = jnp.take(matrix, pivot_rows, axis=0)
    initial = matrix[:width]
    target = jnp.where(moved, pivot_rows, total_rows).astype(jnp.int32)
    swapped = matrix.at[target].set(initial, mode="drop")
    upper = jnp.dot(inverse_lower, picked, precision=lax.Precision.HIGHEST, preferred_element_type=jnp.float32)
    product = jnp.dot(panel_t.T, upper, precision=lax.Precision.HIGHEST, preferred_element_type=jnp.float32)
    updated = swapped - product
    updated = updated.at[:width].set(upper)
    return updated
```

```python
import functools

import jax
import jax.numpy as jnp
from jax import lax
from jax.experimental import pallas as pl
from jax.experimental.pallas import tpu as pltpu
from jax.sharding import PartitionSpec as P

MESH = pl.DeviceIdType.MESH
F32, BF16 = jnp.float32, jnp.bfloat16

NX, NY, NZ = 8, 8, 8
SLOTS = 32
CHUNKS = 4


def order_of(n):
    order = [0]
    for d in range(1, n // 2 + 1):
        order.append(d)
        if d <= (n - 1) // 2:
            order.append(-d)
    return order


def groups_of(n):
    order = order_of(n)
    top = n // 2
    groups = [(0, 1, 0)]
    d = 1
    while d <= top:
        last = top if (d + 1 == top and n % 2 == 0) else d
        slots = [i for i, o in enumerate(order) if d <= abs(o) <= last]
        groups.append((slots[0], len(slots), last))
        d = last + 1
    return groups


def split2(v):
    hi = v.astype(BF16)
    return hi, (v - hi.astype(F32)).astype(BF16)


def split3(v):
    hi = v.astype(BF16)
    rest = v - hi.astype(F32)
    mid = rest.astype(BF16)
    return hi, mid, (rest - mid.astype(F32)).astype(BF16)


def dot(a, b):
    return jnp.dot(a, b, preferred_element_type=F32)


def dot_t(a, b):
    return lax.dot_general(a, b, (((0,), (0,)), ((), ())), preferred_element_type=F32)


def select(onehot, v):
    hi, mid, lo = split3(v)
    return dot(onehot, hi) + dot(onehot, mid) + dot(onehot, lo)


def lane_iota(shape):
    return lax.broadcasted_iota(jnp.int32, shape, 1).astype(F32)


def sub_iota(shape):
    return lax.broadcasted_iota(jnp.int32, shape, 0).astype(F32)


def onehot(test):
    return jnp.where(test, 1.0, 0.0)


def kernel(
    mat_any, pan_any, inv_any, piv_ref, out_any,
    mat, inv, inv_rel, buf_a, buf_b, work, init, lpe_hi, lpe_lo, up_a, up_b,
    local_sem, send_a, send_b, a1, a2, b1, b2,
    zs, zr, zps, zpr, us, ur, ups, upr, ims, imr, ifs, ifr, out_sem,
):
    rows, cols = mat.shape
    width = inv.shape[0]
    half_rows = rows // 2
    free = width // 2
    n_row = 2 * NZ
    cls_rows = free // 2
    chunk = cls_rows // CHUNKS
    row, col = lax.axis_index("row"), lax.axis_index("col")
    z, core = row // 2, row % 2
    x, y = col // NY, col % NY
    s = 1 - 2 * core

    def at_x(d):
        return (row, lax.rem(x + d + 2 * NX, NX) * NY + y)

    def at_y(d):
        return (row, x * NY + lax.rem(y + d + 2 * NY, NY))

    def at_z(d):
        return (lax.rem(z + d + 2 * NZ, NZ) * 2 + core, col)

    partner = (z * 2 + 1 - core, col)

    barrier = pltpu.get_barrier_semaphore()
    for other in (at_x(1), at_x(-1), at_y(1), at_y(-1), at_z(1), at_z(-1), partner):
        pl.semaphore_signal(barrier, inc=1, device_id=other, device_id_type=MESH)

    half = pan_any.shape[1] // 2
    loads = [
        pltpu.make_async_copy(mat_any, mat, local_sem.at[0]),
        pltpu.make_async_copy(pan_any.at[:, 0:half], buf_a.at[0:8], local_sem.at[1]),
        pltpu.make_async_copy(pan_any.at[:, half:], buf_b.at[0:8], local_sem.at[2]),
        pltpu.make_async_copy(inv_any, inv, local_sem.at[3]),
    ]
    for load in loads:
        load.start()

    p = piv_ref[...].astype(F32)
    place = lane_iota(p.shape)
    moved = p != place
    owner = jnp.floor((p + 0.5) * (1.0 / rows))
    local_row = p - owner * rows
    cls = jnp.where(moved, owner, 0.0)
    member = onehot(jnp.broadcast_to(cls, (n_row, width)) == sub_iota((n_row, width)))
    before = onehot(sub_iota((width, width)) < lane_iota((width, width))).astype(BF16)
    counts = dot(member.astype(BF16), before)
    rank = jnp.sum(member * counts, axis=0, keepdims=True)
    g = jnp.where(moved, free + SLOTS * owner + rank, rank)

    mine = onehot(
        jnp.broadcast_to(g, (SLOTS, width))
        == sub_iota((SLOTS, width)) + (free + SLOTS * row).astype(F32)
    )
    spot = jnp.sum(mine * local_row, axis=1, keepdims=True)
    used = jnp.sum(mine, axis=1, keepdims=True)
    spot = jnp.where(used > 0.0, spot, -1.0)
    pick = onehot(jnp.broadcast_to(spot, (SLOTS, rows)) == lane_iota((SLOTS, rows))).astype(BF16)

    own_slots = pl.ds(pl.multiple_of(free + SLOTS * row, SLOTS), SLOTS)
    loads[0].wait()
    work[own_slots, :] = select(pick, mat[...])

    is_root = row == 0

    @pl.when(is_root)
    def _():
        head = mat[0:width, :]
        unmoved = onehot(jnp.broadcast_to(g, (free, width)) == sub_iota((free, width))).astype(BF16)
        work[0:free, :] = select(unmoved, head)
        owner_z = jnp.floor((owner + 0.5) * 0.5)
        owner_c = owner - 2.0 * owner_z
        reach = jnp.where(owner_c == 0.0, owner_z, NZ - owner_z)
        reach = jnp.where(reach >= NZ, 0.0, reach)
        goal = jnp.where(moved, (owner_c * NZ + reach) * SLOTS + rank, -1.0)
        total = n_row * SLOTS
        send_to = onehot(jnp.broadcast_to(goal, (total, width)) == sub_iota((total, width))).astype(BF16)
        init[...] = select(send_to, head)

    for load in loads[1:]:
        load.wait()
    pl.semaphore_wait(barrier, 7)

    def send(src, dst, ss, rs, to):
        c = pltpu.make_async_remote_copy(
            src_ref=src, dst_ref=dst, send_sem=ss, recv_sem=rs, device_id=to, device_id_type=MESH
        )
        c.start()
        return c

    def recv(ref, sem):
        pltpu.make_async_copy(ref, ref, sem).wait()

    ox, oy, oz = order_of(NX), order_of(NY), order_of(NZ)

    class Half:
        def __init__(self, buf, first, second, n_in, n_out, at_in, at_out, send_sem):
            self.buf, self.first, self.second = buf, first, second
            self.n_in, self.n_out = n_in, n_out
            self.at_in, self.at_out = at_in, at_out
            self.o_in, self.o_out = order_of(n_in), order_of(n_out)
            self.groups = groups_of(n_in)
            self.send_sem = send_sem

        def span(self, o, i0, n):
            base = (self.o_out.index(o) * self.n_in + i0) * 8
            return self.buf.at[base:base + n * 8]

        def next_ones(self, d, n):
            out = []
            if 0 <= d < n // 2:
                out.append(d + 1)
            if 0 >= d > -((n - 1) // 2):
                out.append(d - 1)
            return out

        def inner_from(self, d):
            i = self.o_in.index(d)
            for t in self.next_ones(d, self.n_in):
                j = self.o_in.index(t)
                step = 1 if t > 0 else -1
                send(self.span(0, i, 1), self.span(0, j, 1), self.send_sem, self.first.at[j], self.at_in(step * s))

        def outer_from(self, o, k):
            i0, n, _ = self.groups[k]
            for t in self.next_ones(o, self.n_out):
                step = 1 if t > 0 else -1
                send(
                    self.span(o, i0, n), self.span(t, i0, n), self.send_sem,
                    self.second.at[self.o_out.index(t), k], self.at_out(step * s),
                )

        def inner_round(self, h):
            for d in (h, -h):
                if d in self.o_in:
                    i = self.o_in.index(d)
                    recv(self.span(0, i, 1), self.first.at[i])
                    self.inner_from(d)
            for k, (_, _, hops) in enumerate(self.groups):
                if hops == h:
                    self.outer_from(0, k)

        def outer_round(self, h):
            for k, (i0, n, hops) in enumerate(self.groups):
                for o in (h - hops, hops - h):
                    if o != 0 and h > hops and o in self.o_out:
                        recv(self.span(o, i0, n), self.second.at[self.o_out.index(o), k])
                        self.outer_from(o, k)

        def finish(self):
            ref = self.buf.at[0:(self.n_in * self.n_out - 1) * 8]
            pltpu.make_async_copy(ref, ref, self.send_sem).wait()

    half_a = Half(buf_a, a1, a2, NY, NX, at_y, at_x, send_a.at[0])
    half_b = Half(buf_b, b1, b2, NX, NY, at_x, at_y, send_b.at[0])
    for h in (half_a, half_b):
        h.outer_from(0, 0)
        h.inner_from(0)

    fwd, bwd = NZ // 2, (NZ - 1) // 2

    def slot_rows(d):
        src = lax.rem(z - s * d + 2 * NZ, NZ) * 2 + core
        return work.at[pl.ds(pl.multiple_of(free + SLOTS * src, SLOTS), SLOTS)]

    def partner_rows(d):
        src = lax.rem(z + s * d + 2 * NZ, NZ) * 2 + 1 - core
        return work.at[pl.ds(pl.multiple_of(free + SLOTS * src, SLOTS), SLOTS)]

    z_sends = []

    def slots_from(d):
        ref = slot_rows(d)
        if 0 <= d < fwd:
            j = oz.index(d + 1)
            z_sends.append(send(ref, ref, zs.at[j], zr.at[j], at_z(s)))
        if 0 >= d > -bwd:
            j = oz.index(d - 1)
            z_sends.append(send(ref, ref, zs.at[j], zr.at[j], at_z(-s)))
        i = oz.index(d)
        z_sends.append(send(ref, ref, zps.at[i], zpr.at[i], partner))

    df = lax.rem(s * z + NZ, NZ)
    on_fwd = df <= fwd
    dist = jnp.where(on_fwd, df, NZ - df)
    is_second = (z == 0) & (core == 1)
    source = z == 0
    relays_u = jnp.logical_not(source) & (((df < fwd) & on_fwd) | (jnp.logical_not(on_fwd) & (dist < bwd)))
    ahead = jnp.where(on_fwd, s, -s)

    def u_rows(c, k):
        return work.at[pl.ds(pl.multiple_of(c * cls_rows + k * chunk, chunk), chunk)]

    def u_copy(ref, way, slot, k):
        return pltpu.make_async_remote_copy(
            src_ref=ref, dst_ref=ref, send_sem=us.at[slot, k], recv_sem=ur.at[k],
            device_id=at_z(way), device_id_type=MESH,
        )

    def u_partner(ref, k):
        return pltpu.make_async_remote_copy(
            src_ref=ref, dst_ref=ref, send_sem=ups.at[k], recv_sem=upr.at[k],
            device_id=partner, device_id_type=MESH,
        )

    def u_second(k):
        ref = u_rows(1, k)
        return pltpu.make_async_remote_copy(
            src_ref=ref, dst_ref=ref, send_sem=us.at[2, k], recv_sem=ur.at[k],
            device_id=partner, device_id_type=MESH,
        )

    def i_rows(c, q):
        return init.at[pl.ds(pl.multiple_of((c * NZ + q) * SLOTS, SLOTS), SLOTS)]

    def i_copy(q, way):
        ref = i_rows(core, q)
        return pltpu.make_async_remote_copy(
            src_ref=ref, dst_ref=ref, send_sem=ifs.at[q], recv_sem=ifr.at[q],
            device_id=at_z(way), device_id_type=MESH,
        )

    def i_second():
        ref = init.at[NZ * SLOTS:2 * NZ * SLOTS]
        return pltpu.make_async_remote_copy(
            src_ref=ref, dst_ref=ref, send_sem=ims.at[0], recv_sem=imr.at[0],
            device_id=partner, device_id_type=MESH,
        )

    def i_source_sends(act):
        for q in sorted(range(1, NZ), key=lambda v: -min(v, NZ - v)):
            act(i_copy(q, s if q <= fwd else -s))

    @pl.when(is_root)
    def _():
        for k in range(CHUNKS):
            u_second(k).start()
            u_copy(u_rows(0, k), s, 0, k).start()
            if bwd:
                u_copy(u_rows(0, k), -s, 1, k).start()

    slots_from(0)

    @pl.when(is_root)
    def _():
        for k in range(CHUNKS):
            u_partner(u_rows(0, k), k).start()
        i_second().start()
        i_source_sends(lambda c: c.start())

    for ia, a in enumerate(ox):
        for ib, b in enumerate(oy):
            src = (lax.rem(x - s * a + 2 * NX, NX) * NY + lax.rem(y - s * b + 2 * NY, NY)) * 8
            dst = (ia * NY + ib) * 8
            inv_rel[dst:dst + 8, :] = inv[pl.ds(pl.multiple_of(src, 8), 8), :]
    parts = [g[:, i * 128:(i + 1) * 128] for i in range(width // 128)]
    while len(parts) < 8:
        parts = parts + parts
    flipped = jnp.concatenate(parts[:8], axis=0).T
    g_col = jnp.concatenate([flipped[:, i:i + 1] for i in range(width // 128)], axis=0)
    depth = work.shape[0]
    place_of = onehot(jnp.broadcast_to(g_col, (width, depth)) == lane_iota((width, depth))).astype(BF16)
    inv_hi, inv_lo = split2(inv_rel[...])
    lpe_hi[...] = dot(inv_hi, place_of).astype(BF16)
    lpe_lo[...] = dot(inv_lo, place_of).astype(BF16)

    hops = max(NX // 2 + NY // 2, fwd + CHUNKS, 4 + fwd)
    for h in range(1, hops + 1):
        for hf in (half_a, half_b):
            hf.inner_round(h)
        for hf in (half_a, half_b):
            hf.outer_round(h)
        for d in (h, -h):
            if d in oz:
                recv(slot_rows(d), zr.at[oz.index(d)])
                slots_from(d)

        k = h - 1 - dist

        @pl.when((k >= 0) & (k < CHUNKS) & jnp.logical_not(is_root))
        def _():
            ref = u_rows(core, k)
            recv(ref, ur.at[k])

            @pl.when(is_second)
            def _():
                u_copy(ref, s, 0, k).start()
                if bwd:
                    u_copy(ref, -s, 1, k).start()

            @pl.when(relays_u)
            def _():
                u_copy(ref, ahead, 0, k).start()

            @pl.when(jnp.logical_not(is_second))
            def _():
                u_partner(ref, k).start()

        if h == 4:
            @pl.when(is_second)
            def _():
                ref = init.at[NZ * SLOTS:2 * NZ * SLOTS]
                recv(ref, imr.at[0])
                i_source_sends(lambda c: c.start())

        m = h - 4 - dist

        @pl.when((m >= 0) & jnp.logical_not(source) & on_fwd & (fwd - m >= df))
        def _():
            q = fwd - m
            recv(i_rows(core, q), ifr.at[q])

            @pl.when(q > df)
            def _():
                i_copy(q, s).start()

        @pl.when((m >= 0) & jnp.logical_not(on_fwd) & (NZ - bwd + m <= df))
        def _():
            q = NZ - bwd + m
            recv(i_rows(core, q), ifr.at[q])

            @pl.when(q < df)
            def _():
                i_copy(q, -s).start()

    for d in oz:
        recv(partner_rows(d), zpr.at[oz.index(d)])

    @pl.when(jnp.logical_not(is_root))
    def _():
        for k in range(CHUNKS):
            recv(u_rows(1 - core, k), upr.at[k])

    w_hi, w_lo = split2(work[...])
    upper = dot(lpe_hi[...], w_hi) + dot(lpe_hi[...], w_lo) + dot(lpe_lo[...], w_hi)
    up_a[...] = upper
    for ia in range(NX):
        for ib in range(NY):
            src, dst = (ia * NY + ib) * 8, (ib * NX + ia) * 8
            up_b[dst:dst + 8, :] = up_a[src:src + 8, :]

    mine_init = init[pl.ds(pl.multiple_of((core * NZ + df) * SLOTS, SLOTS), SLOTS), :]
    parts = split3(mine_init)
    ones = jnp.ones((SLOTS, 128), BF16)
    for n, (buf, up) in enumerate(((buf_a, up_a), (buf_b, up_b))):
        u_hi, u_lo = split2(up[...])
        p_hi, p_lo = split2(buf[...])
        product = dot_t(p_hi, u_hi) + dot_t(p_hi, u_lo) + dot_t(p_lo, u_hi)
        at = slice(n * half_rows, (n + 1) * half_rows)
        place = pick[:, at]
        taken = dot_t(place, ones)
        taken = jnp.concatenate([taken] * (cols // 128), axis=1)
        new = dot_t(place, parts[0]) + dot_t(place, parts[1]) + dot_t(place, parts[2])
        mat[at, :] = jnp.where(taken > 0.5, new, mat[at, :]) - product

    @pl.when(is_root)
    def _():
        for ia, a in enumerate(ox):
            for ib, b in enumerate(oy):
                dst = (lax.rem(x - s * a + 2 * NX, NX) * NY + lax.rem(y - s * b + 2 * NY, NY)) * 8
                src = (ia * NY + ib) * 8
                mat[pl.ds(pl.multiple_of(dst, 8), 8), :] = up_a[src:src + 8, :]

    store = pltpu.make_async_copy(mat, out_any, out_sem.at[0])
    store.start()
    half_a.finish()
    half_b.finish()
    for c in z_sends:
        c.wait_send()

    @pl.when(is_root)
    def _():
        for k in range(CHUNKS):
            u_second(k).wait_send()
            u_copy(u_rows(0, k), s, 0, k).wait_send()
            if bwd:
                u_copy(u_rows(0, k), -s, 1, k).wait_send()
            u_partner(u_rows(0, k), k).wait_send()
        i_second().wait_send()
        i_source_sends(lambda c: c.wait_send())

    @pl.when(is_second)
    def _():
        for k in range(CHUNKS):
            u_copy(u_rows(1, k), s, 0, k).wait_send()
            if bwd:
                u_copy(u_rows(1, k), -s, 1, k).wait_send()
        i_source_sends(lambda c: c.wait_send())

    @pl.when(relays_u)
    def _():
        for k in range(CHUNKS):
            u_copy(u_rows(core, k), ahead, 0, k).wait_send()

    @pl.when(jnp.logical_not(source))
    def _():
        for k in range(CHUNKS):
            u_partner(u_rows(core, k), k).wait_send()

    for q in range(1, NZ):
        if q <= fwd:
            @pl.when(jnp.logical_not(source) & on_fwd & (q > df))
            def _():
                i_copy(q, s).wait_send()
        else:
            @pl.when(jnp.logical_not(on_fwd) & (q < df))
            def _():
                i_copy(q, -s).wait_send()

    store.wait()


def local(matrix, panel_t, inverse_lower, pivot_rows):
    rows, cols = matrix.shape
    width = inverse_lower.shape[0]
    depth = width // 2 + 2 * NZ * SLOTS
    half = panel_t.shape[1] // 2
    anywhere = pl.BlockSpec(memory_space=pl.ANY)
    dma = pltpu.SemaphoreType.DMA
    return pl.pallas_call(
        kernel,
        out_shape=jax.ShapeDtypeStruct((rows, cols), F32),
        in_specs=[anywhere, anywhere, anywhere, pl.BlockSpec(memory_space=pltpu.VMEM)],
        out_specs=anywhere,
        scratch_shapes=[
            pltpu.VMEM((rows, cols), F32),
            pltpu.VMEM((width, width), F32),
            pltpu.VMEM((width, width), F32),
            pltpu.VMEM((width, half), F32),
            pltpu.VMEM((width, half), F32),
            pltpu.VMEM((depth, cols), F32),
            pltpu.VMEM((2 * NZ * SLOTS, cols), F32),
            pltpu.VMEM((width, depth), BF16),
            pltpu.VMEM((width, depth), BF16),
            pltpu.VMEM((width, cols), F32),
            pltpu.VMEM((width, cols), F32),
            dma((4,)), dma((1,)), dma((1,)),
            dma((NY,)), dma((NX, len(groups_of(NY)))),
            dma((NX,)), dma((NY, len(groups_of(NX)))),
            dma((NZ,)), dma((NZ,)), dma((NZ,)), dma((NZ,)),
            dma((3, CHUNKS)), dma((CHUNKS,)), dma((CHUNKS,)), dma((CHUNKS,)),
            dma((1,)), dma((1,)), dma((NZ,)), dma((NZ,)), dma((1,)),
        ],
        compiler_params=pltpu.CompilerParams(
            collective_id=0, has_side_effects=True, vmem_limit_bytes=60 << 20
        ),
    )(matrix, panel_t, inverse_lower, pivot_rows.reshape(1, width))


def solution(mesh):
    in_specs = (P("row", "col"), P("col", "row"), P(), P())
    out_specs = P("row", "col")
    return jax.shard_map(local, mesh=mesh, in_specs=in_specs, out_specs=out_specs, check_vma=False)
```

```python
import functools

import jax
import jax.numpy as jnp
from jax import lax
from jax.experimental import pallas as pl
from jax.experimental.pallas import tpu as pltpu
from jax.sharding import PartitionSpec as P

MESH = pl.DeviceIdType.MESH
F32, BF16 = jnp.float32, jnp.bfloat16

NX, NY, NZ = 8, 8, 8
SLOTS = 32


def order_of(n):
    order = [0]
    for d in range(1, n // 2 + 1):
        order.append(d)
        if d <= (n - 1) // 2:
            order.append(-d)
    return order


def groups_of(n):
    order = order_of(n)
    top = n // 2
    groups = [(0, 1, 0)]
    d = 1
    while d <= top:
        last = top if (d + 1 == top and n % 2 == 0) else d
        slots = [i for i, o in enumerate(order) if d <= abs(o) <= last]
        groups.append((slots[0], len(slots), last))
        d = last + 1
    return groups


def split2(v):
    hi = v.astype(BF16)
    return hi, (v - hi.astype(F32)).astype(BF16)


def split3(v):
    hi = v.astype(BF16)
    rest = v - hi.astype(F32)
    mid = rest.astype(BF16)
    return hi, mid, (rest - mid.astype(F32)).astype(BF16)


def dot(a, b):
    return jnp.dot(a, b, preferred_element_type=F32)


def dot_t(a, b):
    return lax.dot_general(a, b, (((0,), (0,)), ((), ())), preferred_element_type=F32)


def select(onehot, v):
    hi, mid, lo = split3(v)
    return dot(onehot, hi) + dot(onehot, mid) + dot(onehot, lo)


def lane_iota(shape):
    return lax.broadcasted_iota(jnp.int32, shape, 1).astype(F32)


def sub_iota(shape):
    return lax.broadcasted_iota(jnp.int32, shape, 0).astype(F32)


def onehot(test):
    return jnp.where(test, 1.0, 0.0)


def kernel(
    mat_any, pan_any, inv_any, piv_ref, out_any,
    mat, inv, inv_rel, buf_a, buf_b, pan_b, work, init, lpe_hi, lpe_lo, w_hi, w_lo, up,
    local_sem, send_a, send_b, a1, a2, b1, b2,
    zs, zr, zps, zpr, us, ur, ups, upr, ims, imr, ifs, ifr, ready, pready, out_sem,
):
    rows, cols = mat.shape
    width = inv.shape[0]
    free = width // 2
    n_row = 2 * NZ
    cls_rows = free // 2
    row, col = lax.axis_index("row"), lax.axis_index("col")
    z, core = row // 2, row % 2
    x, y = col // NY, col % NY
    s = 1 - 2 * core
    first_core = core == 0

    def at_x(d):
        return (row, lax.rem(x + d + 2 * NX, NX) * NY + y)

    def at_y(d):
        return (row, x * NY + lax.rem(y + d + 2 * NY, NY))

    def at_z(t):
        return (t * 2 + core, col)

    partner = (z * 2 + 1 - core, col)

    barrier = pltpu.get_barrier_semaphore()
    for other in (at_x(1), at_x(-1), at_y(1), at_y(-1)):
        pl.semaphore_signal(barrier, inc=1, device_id=other, device_id_type=MESH)
    for t in range(1, NZ):
        @pl.when(z < t)
        def _():
            pl.semaphore_signal(barrier, inc=1, device_id=at_z(t), device_id_type=MESH)

    @pl.when(first_core)
    def _():
        pl.semaphore_signal(barrier, inc=1, device_id=partner, device_id_type=MESH)

    half = pan_any.shape[1] // 2
    loads = [
        pltpu.make_async_copy(mat_any, mat, local_sem.at[0]),
        pltpu.make_async_copy(pan_any.at[:, 0:half], buf_a.at[0:8], local_sem.at[1]),
        pltpu.make_async_copy(pan_any.at[:, half:], buf_b.at[0:8], local_sem.at[2]),
        pltpu.make_async_copy(inv_any, inv, local_sem.at[3]),
    ]
    for load in loads:
        load.start()

    p = piv_ref[...].astype(F32)
    place = lane_iota(p.shape)
    moved = p != place
    owner = jnp.floor((p + 0.5) * (1.0 / rows))
    local_row = p - owner * rows
    cls = jnp.where(moved, owner, 0.0)
    member = onehot(jnp.broadcast_to(cls, (n_row, width)) == sub_iota((n_row, width)))
    before = onehot(sub_iota((width, width)) < lane_iota((width, width))).astype(BF16)
    counts = dot(member.astype(BF16), before)
    rank = jnp.sum(member * counts, axis=0, keepdims=True)
    g = jnp.where(moved, free + SLOTS * owner + rank, rank)

    mine = onehot(
        jnp.broadcast_to(g, (SLOTS, width))
        == sub_iota((SLOTS, width)) + (free + SLOTS * row).astype(F32)
    )
    spot = jnp.sum(mine * local_row, axis=1, keepdims=True)
    used = jnp.sum(mine, axis=1, keepdims=True)
    spot = jnp.where(used > 0.0, spot, -1.0)
    pick = onehot(jnp.broadcast_to(spot, (SLOTS, rows)) == lane_iota((SLOTS, rows))).astype(BF16)

    def slots(t, c):
        return work.at[pl.ds(pl.multiple_of(free + SLOTS * (2 * t + c), SLOTS), SLOTS)]

    loads[0].wait()
    slots(z, core)[...] = select(pick, mat[...])

    is_root = row == 0
    source = z == 0

    @pl.when(is_root)
    def _():
        head = mat[0:width, :]
        unmoved = onehot(jnp.broadcast_to(g, (free, width)) == sub_iota((free, width))).astype(BF16)
        work[0:free, :] = select(unmoved, head)
        owner_z = jnp.floor((owner + 0.5) * 0.5)
        owner_c = owner - 2.0 * owner_z
        goal = jnp.where(moved, (owner_c * NZ + owner_z) * SLOTS + rank, -1.0)
        total = n_row * SLOTS
        send_to = onehot(jnp.broadcast_to(goal, (total, width)) == sub_iota((total, width))).astype(BF16)
        init[...] = select(send_to, head)

    for load in loads[1:]:
        load.wait()
    pl.semaphore_wait(barrier, 4 + z + core)

    def copy(src, dst, ss, rs, to):
        return pltpu.make_async_remote_copy(
            src_ref=src, dst_ref=dst, send_sem=ss, recv_sem=rs, device_id=to, device_id_type=MESH
        )

    def send(src, dst, ss, rs, to):
        copy(src, dst, ss, rs, to).start()

    def recv(ref, sem):
        pltpu.make_async_copy(ref, ref, sem).wait()

    def own_slots(t):
        ref = slots(z, core)
        return copy(ref, ref, zs.at[t], zr.at[z], at_z(t))

    def pass_slots(t):
        ref = slots(t, core)
        return copy(ref, ref, zps.at[t], zpr.at[t], partner)

    def u_rows(c):
        return work.at[pl.ds(pl.multiple_of(c * cls_rows, cls_rows), cls_rows)]

    def u_copy(t):
        ref = u_rows(core)
        return copy(ref, ref, us.at[t], ur.at[0], at_z(t))

    def u_second():
        ref = u_rows(1)
        return copy(ref, ref, us.at[0], ur.at[0], partner)

    def u_pass():
        ref = u_rows(core)
        return copy(ref, ref, ups.at[0], upr.at[0], partner)

    def i_rows(t):
        return init.at[pl.ds(pl.multiple_of((core * NZ + t) * SLOTS, SLOTS), SLOTS)]

    def i_copy(t):
        return copy(i_rows(t), i_rows(t), ifs.at[t], ifr.at[0], at_z(t))

    i_half = init.at[NZ * SLOTS:2 * NZ * SLOTS]

    def i_second():
        return copy(i_half, i_half, ims.at[0], imr.at[0], partner)

    for t in range(NZ - 1):
        @pl.when(t < z)
        def _():
            pl.semaphore_signal(ready.at[z], inc=1, device_id=at_z(t), device_id_type=MESH)
            own_slots(t).start()

    @pl.when(jnp.logical_not(first_core))
    def _():
        pl.semaphore_signal(pready, inc=1, device_id=partner, device_id_type=MESH)
        pass_slots(z).start()

    ox, oy = order_of(NX), order_of(NY)

    class Half:
        def __init__(self, buf, first, second, n_in, n_out, at_in, at_out, send_sem):
            self.buf, self.first, self.second = buf, first, second
            self.n_in, self.n_out = n_in, n_out
            self.at_in, self.at_out = at_in, at_out
            self.o_in, self.o_out = order_of(n_in), order_of(n_out)
            self.groups = groups_of(n_in)
            self.send_sem = send_sem

        def span(self, o, i0, n):
            base = (self.o_out.index(o) * self.n_in + i0) * 8
            return self.buf.at[base:base + n * 8]

        def next_ones(self, d, n):
            out = []
            if 0 <= d < n // 2:
                out.append(d + 1)
            if 0 >= d > -((n - 1) // 2):
                out.append(d - 1)
            return out

        def inner_from(self, d):
            i = self.o_in.index(d)
            for t in self.next_ones(d, self.n_in):
                j = self.o_in.index(t)
                step = 1 if t > 0 else -1
                send(self.span(0, i, 1), self.span(0, j, 1), self.send_sem, self.first.at[j], self.at_in(step * s))

        def outer_from(self, o, k):
            i0, n, _ = self.groups[k]
            for t in self.next_ones(o, self.n_out):
                step = 1 if t > 0 else -1
                send(
                    self.span(o, i0, n), self.span(t, i0, n), self.send_sem,
                    self.second.at[self.o_out.index(t), k], self.at_out(step * s),
                )

        def inner_round(self, h):
            for d in (h, -h):
                if d in self.o_in:
                    i = self.o_in.index(d)
                    recv(self.span(0, i, 1), self.first.at[i])
                    self.inner_from(d)
            for k, (_, _, hops) in enumerate(self.groups):
                if hops == h:
                    self.outer_from(0, k)

        def outer_round(self, h):
            for k, (i0, n, hops) in enumerate(self.groups):
                for o in (h - hops, hops - h):
                    if o != 0 and h > hops and o in self.o_out:
                        recv(self.span(o, i0, n), self.second.at[self.o_out.index(o), k])
                        self.outer_from(o, k)

        def finish(self):
            ref = self.buf.at[0:(self.n_in * self.n_out - 1) * 8]
            pltpu.make_async_copy(ref, ref, self.send_sem).wait()

    half_a = Half(buf_a, a1, a2, NY, NX, at_y, at_x, send_a.at[0])
    half_b = Half(buf_b, b1, b2, NX, NY, at_x, at_y, send_b.at[0])
    for h in (half_a, half_b):
        h.outer_from(0, 0)
        h.inner_from(0)

    for ia, a in enumerate(ox):
        for ib, b in enumerate(oy):
            src = (lax.rem(x - s * a + 2 * NX, NX) * NY + lax.rem(y - s * b + 2 * NY, NY)) * 8
            dst = (ia * NY + ib) * 8
            inv_rel[dst:dst + 8, :] = inv[pl.ds(pl.multiple_of(src, 8), 8), :]
    parts = [g[:, i * 128:(i + 1) * 128] for i in range(width // 128)]
    while len(parts) < 8:
        parts = parts + parts
    flipped = jnp.concatenate(parts[:8], axis=0).T
    g_col = jnp.concatenate([flipped[:, i:i + 1] for i in range(width // 128)], axis=0)
    depth = work.shape[0]
    place_of = onehot(jnp.broadcast_to(g_col, (width, depth)) == lane_iota((width, depth))).astype(BF16)
    inv_hi, inv_lo = split2(inv_rel[...])
    lpe_hi[...] = dot(inv_hi, place_of).astype(BF16)
    lpe_lo[...] = dot(inv_lo, place_of).astype(BF16)

    for h in range(1, NX // 2 + NY // 2 + 1):
        for hf in (half_a, half_b):
            hf.inner_round(h)
        for hf in (half_a, half_b):
            hf.outer_round(h)

    @pl.when(first_core)
    def _():
        pl.semaphore_wait(pready, 1)

        @pl.when(source)
        def _():
            u_second().start()
            u_pass().start()
            i_second().start()

        pass_slots(z).start()

    @pl.when(jnp.logical_not(is_root))
    def _():
        recv(u_rows(core), ur.at[0])

        @pl.when(jnp.logical_not(source))
        def _():
            u_pass().start()

        @pl.when(source)
        def _():
            recv(i_half, imr.at[0])

    def along_z(lo, hi):
        for t in range(lo, hi):
            @pl.when(z < t)
            def _():
                pl.semaphore_wait(ready.at[t], 1)

                @pl.when(source)
                def _():
                    u_copy(t).start()
                    i_copy(t).start()

                own_slots(t).start()

            @pl.when(z != t)
            def _():
                recv(slots(t, core), zr.at[t])
                pass_slots(t).start()

    def other_core(lo, hi):
        for t in range(lo, hi):
            recv(slots(t, 1 - core), zpr.at[t])

    for ib in range(NY):
        for ia in range(NX):
            src, dst = (ib * NX + ia) * 8, (ia * NY + ib) * 8
            pan_b[dst:dst + 8, :] = buf_b[src:src + 8, :]
    for n, buf in enumerate((buf_a, pan_b)):
        at = slice(n * half, (n + 1) * half)
        p_hi, p_lo = split2(buf[...])
        w = dot_t(p_hi, lpe_hi[...]) + dot_t(p_hi, lpe_lo[...]) + dot_t(p_lo, lpe_hi[...])
        w_hi[at, :], w_lo[at, :] = split2(w)

    cut = free + n_row * SLOTS // 2
    along_z(0, NZ // 2)

    @pl.when(jnp.logical_not(source))
    def _():
        recv(i_rows(z), ifr.at[0])

    @pl.when(jnp.logical_not(is_root))
    def _():
        recv(u_rows(1 - core), upr.at[0])

    other_core(0, NZ // 2)

    def product(l_hi, l_lo, v):
        v_hi, v_lo = split2(v)
        return dot(l_hi, v_hi) + dot(l_hi, v_lo) + dot(l_lo, v_hi)

    parts = split3(i_rows(z)[...])
    ones = jnp.ones((SLOTS, 128), BF16)
    v_hi, v_lo = split2(work[0:cut, :])
    for n in range(2):
        at = slice(n * half, (n + 1) * half)
        place = pick[:, at]
        taken = dot_t(place, ones)
        taken = jnp.concatenate([taken] * (cols // 128), axis=1)
        new = dot_t(place, parts[0]) + dot_t(place, parts[1]) + dot_t(place, parts[2])
        early = dot(w_hi[at, 0:cut], v_hi) + dot(w_hi[at, 0:cut], v_lo) + dot(w_lo[at, 0:cut], v_hi)
        mat[at, :] = jnp.where(taken > 0.5, new, mat[at, :]) - early

    @pl.when(is_root)
    def _():
        up[...] = product(lpe_hi[:, 0:cut], lpe_lo[:, 0:cut], work[0:cut, :])

    along_z(NZ // 2, NZ)
    other_core(NZ // 2, NZ)

    v_hi, v_lo = split2(work[cut:, :])
    for n in range(2):
        at = slice(n * half, (n + 1) * half)
        late = dot(w_hi[at, cut:], v_hi) + dot(w_hi[at, cut:], v_lo) + dot(w_lo[at, cut:], v_hi)
        mat[at, :] = mat[at, :] - late

    @pl.when(is_root)
    def _():
        up[...] += product(lpe_hi[:, cut:], lpe_lo[:, cut:], work[cut:, :])
        for ia, a in enumerate(ox):
            for ib, b in enumerate(oy):
                dst = (lax.rem(x - s * a + 2 * NX, NX) * NY + lax.rem(y - s * b + 2 * NY, NY)) * 8
                src = (ia * NY + ib) * 8
                mat[pl.ds(pl.multiple_of(dst, 8), 8), :] = up[src:src + 8, :]

    store = pltpu.make_async_copy(mat, out_any, out_sem.at[0])
    store.start()
    half_a.finish()
    half_b.finish()
    for t in range(NZ):
        @pl.when(z != t)
        def _():
            own_slots(t).wait_send()

            @pl.when(source)
            def _():
                u_copy(t).wait_send()
                i_copy(t).wait_send()

        pass_slots(t).wait_send()

    @pl.when(is_root)
    def _():
        u_second().wait_send()
        i_second().wait_send()

    @pl.when(jnp.logical_or(is_root, jnp.logical_not(source)))
    def _():
        u_pass().wait_send()

    store.wait()


def local(matrix, panel_t, inverse_lower, pivot_rows):
    rows, cols = matrix.shape
    width = inverse_lower.shape[0]
    depth = width // 2 + 2 * NZ * SLOTS
    half = panel_t.shape[1] // 2
    anywhere = pl.BlockSpec(memory_space=pl.ANY)
    dma, regular = pltpu.SemaphoreType.DMA, pltpu.SemaphoreType.REGULAR
    return pl.pallas_call(
        kernel,
        out_shape=jax.ShapeDtypeStruct((rows, cols), F32),
        in_specs=[anywhere, anywhere, anywhere, pl.BlockSpec(memory_space=pltpu.VMEM)],
        out_specs=anywhere,
        scratch_shapes=[
            pltpu.VMEM((rows, cols), F32),
            pltpu.VMEM((width, width), F32),
            pltpu.VMEM((width, width), F32),
            pltpu.VMEM((width, half), F32),
            pltpu.VMEM((width, half), F32),
            pltpu.VMEM((width, half), F32),
            pltpu.VMEM((depth, cols), F32),
            pltpu.VMEM((2 * NZ * SLOTS, cols), F32),
            pltpu.VMEM((width, depth), BF16),
            pltpu.VMEM((width, depth), BF16),
            pltpu.VMEM((rows, depth), BF16),
            pltpu.VMEM((rows, depth), BF16),
            pltpu.VMEM((width, cols), F32),
            dma((4,)), dma((1,)), dma((1,)),
            dma((NY,)), dma((NX, len(groups_of(NY)))),
            dma((NX,)), dma((NY, len(groups_of(NX)))),
            dma((NZ,)), dma((NZ,)), dma((NZ,)), dma((NZ,)),
            dma((NZ,)), dma((1,)), dma((1,)), dma((1,)),
            dma((1,)), dma((1,)), dma((NZ,)), dma((1,)),
            regular((NZ,)), regular, dma((1,)),
        ],
        compiler_params=pltpu.CompilerParams(
            collective_id=0, has_side_effects=True, vmem_limit_bytes=60 << 20
        ),
    )(matrix, panel_t, inverse_lower, pivot_rows.reshape(1, width))


def solution(mesh):
    in_specs = (P("row", "col"), P("col", "row"), P(), P())
    out_specs = P("row", "col")
    return jax.shard_map(local, mesh=mesh, in_specs=in_specs, out_specs=out_specs, check_vma=False)
```

```python
import functools

import jax
import jax.numpy as jnp
from jax import lax
from jax.experimental import pallas as pl
from jax.experimental.pallas import tpu as pltpu
from jax.sharding import PartitionSpec as P

MESH = pl.DeviceIdType.MESH
UPPER = 99.0
HOP = 3.0
F32, BF16 = jnp.float32, jnp.bfloat16

NX, NY, NZ = 8, 8, 8
SLOTS = 32


def order_of(n):
    order = [0]
    for d in range(1, n // 2 + 1):
        order.append(d)
        if d <= (n - 1) // 2:
            order.append(-d)
    return order


def groups_of(n):
    order = order_of(n)
    top = n // 2
    groups = [(0, 1, 0)]
    d = 1
    while d <= top:
        last = top if (d + 1 == top and n % 2 == 0) else d
        slots = [i for i, o in enumerate(order) if d <= abs(o) <= last]
        groups.append((slots[0], len(slots), last))
        d = last + 1
    return groups


def split2(v):
    hi = v.astype(BF16)
    return hi, (v - hi.astype(F32)).astype(BF16)


def dot(a, b):
    return jnp.dot(a, b, preferred_element_type=F32)


def dot_t(a, b):
    return lax.dot_general(a, b, (((0,), (0,)), ((), ())), preferred_element_type=F32)


def select(onehot, v):
    hi, lo = split2(v)
    return dot(onehot, hi) + dot(onehot, lo)


def lane_iota(shape):
    return lax.broadcasted_iota(jnp.int32, shape, 1).astype(F32)


def sub_iota(shape):
    return lax.broadcasted_iota(jnp.int32, shape, 0).astype(F32)


def onehot(test):
    return jnp.where(test, 1.0, 0.0)


def kernel(
    mat_any, pan_any, inv_any, piv_ref, mat,
    inv, inv_rel, buf_a, buf_b, work, init, lpe_hi, lpe_lo, up, up_b,
    local_sem, send_a, send_b, a1, a2, b1, b2,
    zs, zr, zps, zpr, us, ur, ups, upr, ims, imr, ifs, ifr, ready, pready,
):
    rows, cols = mat.shape
    width = inv.shape[0]
    free = width // 2
    n_row = 2 * NZ
    row, col = lax.axis_index("row"), lax.axis_index("col")
    z, core = row // 2, row % 2
    x, y = col // NY, col % NY
    s = 1 - 2 * core
    first_core = core == 0

    def at_x(d):
        return (row, lax.rem(x + d + 2 * NX, NX) * NY + y)

    def at_y(d):
        return (row, x * NY + lax.rem(y + d + 2 * NY, NY))

    def at_z(t):
        return (t * 2 + core, col)

    partner = (z * 2 + 1 - core, col)

    barrier = pltpu.get_barrier_semaphore()
    for other in [at_x(d) for d in range(1, NX)] + [at_y(d) for d in range(1, NY)]:
        pl.semaphore_signal(barrier, inc=1, device_id=other, device_id_type=MESH)
    for t in range(1, NZ):
        @pl.when(z < t)
        def _():
            pl.semaphore_signal(barrier, inc=1, device_id=at_z(t), device_id_type=MESH)

    @pl.when(first_core)
    def _():
        pl.semaphore_signal(barrier, inc=1, device_id=partner, device_id_type=MESH)

    half = pan_any.shape[1] // 2
    loads = [
        pltpu.make_async_copy(pan_any.at[:, 0:half], buf_a.at[0:8], local_sem.at[0]),
        pltpu.make_async_copy(pan_any.at[:, half:], buf_b.at[0:8], local_sem.at[1]),
        pltpu.make_async_copy(mat_any, mat, local_sem.at[2]),
        pltpu.make_async_copy(inv_any, inv, local_sem.at[3]),
    ]
    for load in loads:
        load.start()

    for load in loads[:2]:
        load.wait()
    pl.semaphore_wait(barrier, NX + NY - 2 + z + core)

    def copy(src, dst, ss, rs, to):
        return pltpu.make_async_remote_copy(
            src_ref=src, dst_ref=dst, send_sem=ss, recv_sem=rs, device_id=to, device_id_type=MESH
        )

    def send(src, dst, ss, rs, to):
        copy(src, dst, ss, rs, to).start()

    def recv(ref, sem):
        pltpu.make_async_copy(ref, ref, sem).wait()

    def slots(t, c):
        return work.at[pl.ds(pl.multiple_of(free + SLOTS * (2 * t + c), SLOTS), SLOTS)]

    is_root = row == 0
    source = z == 0

    def own_slots(t):
        ref = slots(z, core)
        return copy(ref, ref, zs.at[t], zr.at[z], at_z(t))

    def pass_slots(t):
        ref = slots(t, core)
        return copy(ref, ref, zps.at[t], zpr.at[t], partner)

    u_rows = work.at[0:free]

    def u_copy(t):
        return copy(u_rows, u_rows, us.at[t], ur.at[0], at_z(t))

    def u_pass():
        return copy(u_rows, u_rows, ups.at[0], upr.at[0], partner)

    def i_pair(t):
        return init.at[pl.ds(pl.multiple_of(2 * t * SLOTS, 2 * SLOTS), 2 * SLOTS)]

    def i_copy(t):
        return copy(i_pair(t), i_pair(t), ifs.at[t], ifr.at[0], at_z(t))

    def i_rows(c):
        return init.at[pl.ds(pl.multiple_of((2 * z + c) * SLOTS, SLOTS), SLOTS)]

    def i_pass():
        return copy(i_rows(1), i_rows(1), ims.at[0], imr.at[0], partner)

    for t in range(NZ - 1):
        @pl.when(t < z)
        def _():
            pl.semaphore_signal(ready.at[z], inc=1, device_id=at_z(t), device_id_type=MESH)

    @pl.when(jnp.logical_not(first_core))
    def _():
        pl.semaphore_signal(pready, inc=1, device_id=partner, device_id_type=MESH)

    def root_serve(t):
        pl.semaphore_wait(ready.at[t], 1)
        u_copy(t).start()
        i_copy(t).start()
        own_slots(t).start()

    ox, oy = order_of(NX), order_of(NY)

    class Half:
        def __init__(self, buf, first, second, n_in, n_out, at_in, at_out, send_sem):
            self.buf, self.first, self.second = buf, first, second
            self.n_in, self.n_out = n_in, n_out
            self.at_in, self.at_out = at_in, at_out
            self.o_in, self.o_out = order_of(n_in), order_of(n_out)
            self.groups = groups_of(n_in)
            self.send_sem = send_sem

        def span(self, o, i0, n):
            base = (self.o_out.index(o) * self.n_in + i0) * 8
            return self.buf.at[base:base + n * 8]

        def next_ones(self, d, n):
            out = []
            if 0 <= d < n // 2:
                out.append(d + 1)
            if 0 >= d > -((n - 1) // 2):
                out.append(d - 1)
            return out

        def inner_sends(self):
            own = self.span(0, 0, 1)
            for j, d in enumerate(self.o_in):
                if j:
                    send(own, self.span(0, j, 1), self.send_sem, self.first.at[j], self.at_in(d * s))

        def outer_from(self, o, k):
            i0, n, _ = self.groups[k]
            for t in self.next_ones(o, self.n_out):
                step = 1 if t > 0 else -1
                send(
                    self.span(o, i0, n), self.span(t, i0, n), self.send_sem,
                    self.second.at[self.o_out.index(t), k], self.at_out(step * s),
                )

        def arrive(self, o, k):
            i0, n, _ = self.groups[k]
            if o:
                recv(self.span(o, i0, n), self.second.at[self.o_out.index(o), k])
            else:
                for i in range(i0, i0 + n):
                    recv(self.span(0, i, 1), self.first.at[i])
            self.outer_from(o, k)

        def events(self):
            out = []
            for k, (_, _, hops) in enumerate(self.groups):
                for o in self.o_out:
                    if k or o:
                        start = 0.9 + 0.75 * hops if k else 0.0
                        out.append((start + HOP * abs(o), self, o, k))
            return out

        def finish(self):
            ref = self.buf.at[0:(self.n_in * self.n_out - 1) * 8]
            pltpu.make_async_copy(ref, ref, self.send_sem).wait()

    half_a = Half(buf_a, a1, a2, NY, NX, at_y, at_x, send_a.at[0])
    half_b = Half(buf_b, b1, b2, NX, NY, at_x, at_y, send_b.at[0])
    for h in (half_a, half_b):
        h.outer_from(0, 0)
        h.inner_sends()

    p = piv_ref[...].astype(F32)
    place = lane_iota(p.shape)
    moved = p != place
    owner = jnp.floor((p + 0.5) * (1.0 / rows))
    local_row = p - owner * rows
    cls = jnp.where(moved, owner, 0.0)
    member = onehot(jnp.broadcast_to(cls, (n_row, width)) == sub_iota((n_row, width)))
    before = onehot(sub_iota((width, width)) < lane_iota((width, width))).astype(BF16)
    counts = dot(member.astype(BF16), before)
    rank = jnp.sum(member * counts, axis=0, keepdims=True)
    g = jnp.where(moved, free + SLOTS * owner + rank, rank)

    mine = onehot(
        jnp.broadcast_to(g, (SLOTS, width))
        == sub_iota((SLOTS, width)) + (free + SLOTS * row).astype(F32)
    )
    spot = jnp.sum(mine * local_row, axis=1, keepdims=True)
    used = jnp.sum(mine, axis=1, keepdims=True)
    spot = jnp.where(used > 0.0, spot, -1.0)
    pick = onehot(jnp.broadcast_to(spot, (SLOTS, rows)) == lane_iota((SLOTS, rows))).astype(BF16)

    loads[2].wait()
    slots(z, core)[...] = select(pick, mat[...])

    @pl.when(is_root)
    def _():
        head = mat[0:width, :]
        unmoved = onehot(jnp.broadcast_to(g, (free, width)) == sub_iota((free, width))).astype(BF16)
        work[0:free, :] = select(unmoved, head)
        goal = jnp.where(moved, owner * SLOTS + rank, -1.0)
        total = n_row * SLOTS
        send_to = onehot(jnp.broadcast_to(goal, (total, width)) == sub_iota((total, width))).astype(BF16)
        init[...] = select(send_to, head)

    for t in range(NZ - 1):
        @pl.when(t < z)
        def _():
            own_slots(t).start()

    @pl.when(jnp.logical_not(first_core))
    def _():
        pass_slots(z).start()

    @pl.when(first_core)
    def _():
        pl.semaphore_wait(pready, 1)
        pass_slots(z).start()

    @pl.when(is_root)
    def _():
        u_pass().start()
        i_pass().start()
        for t in range(1, NZ // 2 + 1):
            root_serve(t)


    def permute_inverse():
        loads[3].wait()
        for ia, a in enumerate(ox):
            for ib, b in enumerate(oy):
                src = (lax.rem(x - s * a + 2 * NX, NX) * NY + lax.rem(y - s * b + 2 * NY, NY)) * 8
                dst = (ia * NY + ib) * 8
                inv_rel[dst:dst + 8, :] = inv[pl.ds(pl.multiple_of(src, 8), 8), :]
        parts = [g[:, i * 128:(i + 1) * 128] for i in range(width // 128)]
        while len(parts) < 8:
            parts = parts + parts
        flipped = jnp.concatenate(parts[:8], axis=0).T
        g_col = jnp.concatenate([flipped[:, i:i + 1] for i in range(width // 128)], axis=0)
        depth = work.shape[0]
        place_of = onehot(jnp.broadcast_to(g_col, (width, depth)) == lane_iota((width, depth))).astype(BF16)
        inv_hi, inv_lo = split2(inv_rel[...])
        lpe_hi[...] = dot(inv_hi, place_of).astype(BF16)
        lpe_lo[...] = dot(inv_lo, place_of).astype(BF16)

    def serve(q):
        t = z + q

        @pl.when((t < NZ) & jnp.logical_not(is_root))
        def _():
            pl.semaphore_wait(ready.at[t], 1)
            own_slots(t).start()

    def finish_upper():
        far_first = first_core & jnp.logical_not(source)

        @pl.when(far_first)
        def _():
            recv(u_rows, ur.at[0])
            u_pass().start()
            recv(i_pair(z), ifr.at[0])
            i_pass().start()

        def along_z(lo, hi):
            for t in range(lo, hi):
                @pl.when(z != t)
                def _():
                    recv(slots(t, core), zr.at[t])
                    pass_slots(t).start()

        def other_core(lo, hi):
            for t in range(lo, hi):
                recv(slots(t, 1 - core), zpr.at[t])

        along_z(0, NZ)

        @pl.when(jnp.logical_not(first_core))
        def _():
            recv(u_rows, upr.at[0])
            recv(i_rows(1), imr.at[0])

        other_core(0, NZ)

        v_hi, v_lo = split2(work[...])
        up[...] = dot(lpe_hi[...], v_hi) + dot(lpe_hi[...], v_lo) + dot(lpe_lo[...], v_hi)
        for ia in range(NX):
            for ib in range(NY):
                src, dst = (ia * NY + ib) * 8, (ib * NX + ia) * 8
                up_b[dst:dst + 8, :] = up[src:src + 8, :]

    leaves = []
    todo = [e for e in half_a.events() + half_b.events()]
    todo += [(1.5 + 1.05 * q, serve, q, 0) for q in range(1, NZ)]
    todo += [(1.5 * (t - NZ // 2 + 1), root_serve, t, 0) for t in range(NZ // 2 + 1, NZ)]
    todo.append((UPPER, finish_upper, 0, 0))
    todo.append((6.0, permute_inverse, 0, 0))
    for e in sorted(todo, key=lambda e: e[0]):
        _, what, o, k = e
        if what is serve:
            serve(o)
        elif what is root_serve:
            pl.when(is_root)(functools.partial(root_serve, o))
        elif what in (permute_inverse, finish_upper):
            what()
        elif o and not what.next_ones(o, what.n_out):
            leaves.append((what, o, k))
        else:
            what.arrive(o, k)

    parts = split2(i_rows(core)[...])
    ones = jnp.ones((SLOTS, 128), BF16)
    halves = []
    for n, (hf, u) in enumerate(((half_a, up), (half_b, up_b))):
        inner = sum(1 for o in hf.o_out if hf.next_ones(o, hf.n_out)) * hf.n_in * 8
        halves.append((slice(n * half, (n + 1) * half), hf, u, inner))

    def part(hf, u, k):
        p_hi, p_lo = split2(hf.buf[k, :])
        u_hi, u_lo = split2(u[k, :])
        return dot_t(p_hi, u_hi) + dot_t(p_hi, u_lo) + dot_t(p_lo, u_hi)

    for at, hf, u, inner in halves:
        place = pick[:, at]
        taken = dot_t(place, ones)
        taken = jnp.concatenate([taken] * (cols // 128), axis=1)
        new = dot_t(place, parts[0]) + dot_t(place, parts[1])
        mat[at, :] = jnp.where(taken > 0.5, new, mat[at, :]) - part(hf, u, slice(0, inner))

    for hf, o, k in leaves:
        hf.arrive(o, k)

    for at, hf, u, inner in halves:
        mat[at, :] = mat[at, :] - part(hf, u, slice(inner, width))

    @pl.when(is_root)
    def _():
        for ia, a in enumerate(ox):
            for ib, b in enumerate(oy):
                dst = (lax.rem(x - s * a + 2 * NX, NX) * NY + lax.rem(y - s * b + 2 * NY, NY)) * 8
                src = (ia * NY + ib) * 8
                mat[pl.ds(pl.multiple_of(dst, 8), 8), :] = up[src:src + 8, :]

    half_a.finish()
    half_b.finish()
    for t in range(NZ):
        @pl.when(z != t)
        def _():
            own_slots(t).wait_send()

        pass_slots(t).wait_send()

    @pl.when(is_root)
    def _():
        for t in range(1, NZ):
            u_copy(t).wait_send()
            i_copy(t).wait_send()

    @pl.when(first_core)
    def _():
        u_pass().wait_send()
        i_pass().wait_send()


def local(matrix, panel_t, inverse_lower, pivot_rows):
    rows, cols = matrix.shape
    width = inverse_lower.shape[0]
    depth = width // 2 + 2 * NZ * SLOTS
    half = panel_t.shape[1] // 2
    hbm, vmem = pl.BlockSpec(memory_space=pltpu.HBM), pl.BlockSpec(memory_space=pltpu.VMEM)
    dma, regular = pltpu.SemaphoreType.DMA, pltpu.SemaphoreType.REGULAR
    held = [pltpu.with_memory_space_constraint(v, pltpu.HBM) for v in (matrix, panel_t, inverse_lower)]
    return pl.pallas_call(
        kernel,
        out_shape=jax.ShapeDtypeStruct((rows, cols), F32),
        in_specs=[hbm, hbm, hbm, vmem],
        out_specs=vmem,
        scratch_shapes=[
            pltpu.VMEM((width, width), F32),
            pltpu.VMEM((width, width), F32),
            pltpu.VMEM((width, half), F32),
            pltpu.VMEM((width, half), F32),
            pltpu.VMEM((depth, cols), F32),
            pltpu.VMEM((2 * NZ * SLOTS, cols), F32),
            pltpu.VMEM((width, depth), BF16),
            pltpu.VMEM((width, depth), BF16),
            pltpu.VMEM((width, cols), F32),
            pltpu.VMEM((width, cols), F32),
            dma((4,)), dma((1,)), dma((1,)),
            dma((NY,)), dma((NX, len(groups_of(NY)))),
            dma((NX,)), dma((NY, len(groups_of(NX)))),
            dma((NZ,)), dma((NZ,)), dma((NZ,)), dma((NZ,)),
            dma((NZ,)), dma((1,)), dma((1,)), dma((1,)),
            dma((1,)), dma((1,)), dma((NZ,)), dma((1,)),
            regular((NZ,)), regular,
        ],
        compiler_params=pltpu.CompilerParams(
            collective_id=0, has_side_effects=True, vmem_limit_bytes=20 << 20
        ),
    )(*held, pivot_rows.reshape(1, width))


def solution(mesh):
    in_specs = (P("row", "col"), P("col", "row"), P(), P())
    out_specs = P("row", "col")
    return jax.shard_map(local, mesh=mesh, in_specs=in_specs, out_specs=out_specs, check_vma=False)
```

```python
import functools

import jax
import jax.numpy as jnp
from jax import lax
from jax.experimental import pallas as pl
from jax.experimental.pallas import tpu as pltpu
from jax.sharding import PartitionSpec as P

MESH = pl.DeviceIdType.MESH
UPPER = 99.0
HOP = 3.0
F32, BF16 = jnp.float32, jnp.bfloat16

NX, NY, NZ = 8, 8, 8
SLOTS = 32


def order_of(n):
    order = [0]
    for d in range(1, n // 2 + 1):
        order.append(d)
        if d <= (n - 1) // 2:
            order.append(-d)
    return order


def groups_of(n):
    order = order_of(n)
    top = n // 2
    groups = [(0, 1, 0)]
    d = 1
    while d <= top:
        last = top if (d + 1 == top and n % 2 == 0) else d
        slots = [i for i, o in enumerate(order) if d <= abs(o) <= last]
        groups.append((slots[0], len(slots), last))
        d = last + 1
    return groups


def split2(v):
    hi = v.astype(BF16)
    return hi, (v - hi.astype(F32)).astype(BF16)


def dot(a, b):
    return jnp.dot(a, b, preferred_element_type=F32)


def dot_t(a, b):
    return lax.dot_general(a, b, (((0,), (0,)), ((), ())), preferred_element_type=F32)


def select(onehot, v):
    hi, lo = split2(v)
    return dot(onehot, hi) + dot(onehot, lo)


def lane_iota(shape):
    return lax.broadcasted_iota(jnp.int32, shape, 1).astype(F32)


def sub_iota(shape):
    return lax.broadcasted_iota(jnp.int32, shape, 0).astype(F32)


def onehot(test):
    return jnp.where(test, 1.0, 0.0)


def kernel(
    mat_any, pan_any, inv_any, piv_ref, mat,
    inv, inv_rel, buf_a, buf_b, work, init, lpe_hi, lpe_lo, up, up_b,
    local_sem, send_a, send_b, a1, a2, b1, b2,
    zs, zr, zps, zpr, us, ur, ups, upr, ims, imr, ifs, ifr, ready, pready,
):
    rows, cols = mat.shape
    width = inv.shape[0]
    free = width // 2
    n_row = 2 * NZ
    row, col = lax.axis_index("row"), lax.axis_index("col")
    z, core = row // 2, row % 2
    x, y = col // NY, col % NY
    s = 1 - 2 * core
    first_core = core == 0

    def at_x(d):
        return (row, lax.rem(x + d + 2 * NX, NX) * NY + y)

    def at_y(d):
        return (row, x * NY + lax.rem(y + d + 2 * NY, NY))

    def at_z(t):
        return (t * 2 + core, col)

    partner = (z * 2 + 1 - core, col)

    barrier = pltpu.get_barrier_semaphore()
    for other in [at_x(d) for d in range(1, NX)] + [at_y(d) for d in range(1, NY)]:
        pl.semaphore_signal(barrier, inc=1, device_id=other, device_id_type=MESH)
    for t in range(1, NZ):
        @pl.when(z < t)
        def _():
            pl.semaphore_signal(barrier, inc=1, device_id=at_z(t), device_id_type=MESH)

    @pl.when(first_core)
    def _():
        pl.semaphore_signal(barrier, inc=1, device_id=partner, device_id_type=MESH)

    half = pan_any.shape[1] // 2
    loads = [
        pltpu.make_async_copy(pan_any.at[:, 0:half], buf_a.at[0:8], local_sem.at[0]),
        pltpu.make_async_copy(pan_any.at[:, half:], buf_b.at[0:8], local_sem.at[1]),
        pltpu.make_async_copy(mat_any, mat, local_sem.at[2]),
        pltpu.make_async_copy(inv_any, inv, local_sem.at[3]),
    ]
    for load in loads:
        load.start()

    for load in loads[:2]:
        load.wait()
    pl.semaphore_wait(barrier, NX + NY - 2 + z + core)

    def copy(src, dst, ss, rs, to):
        return pltpu.make_async_remote_copy(
            src_ref=src, dst_ref=dst, send_sem=ss, recv_sem=rs, device_id=to, device_id_type=MESH
        )

    def send(src, dst, ss, rs, to):
        copy(src, dst, ss, rs, to).start()

    def recv(ref, sem):
        pltpu.make_async_copy(ref, ref, sem).wait()

    def slots(t, c):
        return work.at[pl.ds(pl.multiple_of(free + SLOTS * (2 * t + c), SLOTS), SLOTS)]

    is_root = row == 0
    source = z == 0

    def own_slots(t):
        ref = slots(z, core)
        return copy(ref, ref, zs.at[t], zr.at[z], at_z(t))

    def pass_slots(t):
        ref = slots(t, core)
        return copy(ref, ref, zps.at[t], zpr.at[t], partner)

    u_rows = work.at[0:free]

    def u_copy(t):
        return copy(u_rows, u_rows, us.at[t], ur.at[0], at_z(t))

    def u_pass():
        return copy(u_rows, u_rows, ups.at[0], upr.at[0], partner)

    def i_pair(t):
        return init.at[pl.ds(pl.multiple_of(2 * t * SLOTS, 2 * SLOTS), 2 * SLOTS)]

    def i_copy(t):
        return copy(i_pair(t), i_pair(t), ifs.at[t], ifr.at[0], at_z(t))

    def i_rows(c):
        return init.at[pl.ds(pl.multiple_of((2 * z + c) * SLOTS, SLOTS), SLOTS)]

    def i_pass():
        return copy(i_rows(1), i_rows(1), ims.at[0], imr.at[0], partner)

    for t in range(NZ - 1):
        @pl.when(t < z)
        def _():
            pl.semaphore_signal(ready.at[z], inc=1, device_id=at_z(t), device_id_type=MESH)

    @pl.when(jnp.logical_not(first_core))
    def _():
        pl.semaphore_signal(pready, inc=1, device_id=partner, device_id_type=MESH)

    def root_serve(t):
        pl.semaphore_wait(ready.at[t], 1)
        u_copy(t).start()
        i_copy(t).start()
        own_slots(t).start()

    ox, oy = order_of(NX), order_of(NY)

    class Half:
        def __init__(self, buf, first, second, n_in, n_out, at_in, at_out, send_sem):
            self.buf, self.first, self.second = buf, first, second
            self.n_in, self.n_out = n_in, n_out
            self.at_in, self.at_out = at_in, at_out
            self.o_in, self.o_out = order_of(n_in), order_of(n_out)
            self.groups = groups_of(n_in)
            self.send_sem = send_sem

        def span(self, o, i0, n):
            base = (self.o_out.index(o) * self.n_in + i0) * 8
            return self.buf.at[base:base + n * 8]

        def next_ones(self, d, n):
            out = []
            if 0 <= d < n // 2:
                out.append(d + 1)
            if 0 >= d > -((n - 1) // 2):
                out.append(d - 1)
            return out

        def inner_sends(self):
            own = self.span(0, 0, 1)
            for j, d in enumerate(self.o_in):
                if j:
                    send(own, self.span(0, j, 1), self.send_sem, self.first.at[j], self.at_in(d * s))

        def outer_from(self, o, k):
            i0, n, _ = self.groups[k]
            for t in self.next_ones(o, self.n_out):
                step = 1 if t > 0 else -1
                send(
                    self.span(o, i0, n), self.span(t, i0, n), self.send_sem,
                    self.second.at[self.o_out.index(t), k], self.at_out(step * s),
                )

        def arrive(self, o, k):
            i0, n, _ = self.groups[k]
            if o:
                recv(self.span(o, i0, n), self.second.at[self.o_out.index(o), k])
            else:
                for i in range(i0, i0 + n):
                    recv(self.span(0, i, 1), self.first.at[i])
            self.outer_from(o, k)

        def events(self):
            out = []
            for k, (_, _, hops) in enumerate(self.groups):
                for o in self.o_out:
                    if k or o:
                        start = 0.9 + 0.75 * hops if k else 0.0
                        out.append((start + HOP * abs(o), self, o, k))
            return out

        def finish(self):
            ref = self.buf.at[0:(self.n_in * self.n_out - 1) * 8]
            pltpu.make_async_copy(ref, ref, self.send_sem).wait()

    half_a = Half(buf_a, a1, a2, NY, NX, at_y, at_x, send_a.at[0])
    half_b = Half(buf_b, b1, b2, NX, NY, at_x, at_y, send_b.at[0])
    for h in (half_a, half_b):
        h.outer_from(0, 0)
        h.inner_sends()

    p = piv_ref[...].astype(F32)
    place = lane_iota(p.shape)
    moved = p != place
    owner = jnp.floor((p + 0.5) * (1.0 / rows))
    local_row = p - owner * rows
    cls = jnp.where(moved, owner, 0.0)
    member = onehot(jnp.broadcast_to(cls, (n_row, width)) == sub_iota((n_row, width)))
    before = onehot(sub_iota((width, width)) < lane_iota((width, width))).astype(BF16)
    counts = dot(member.astype(BF16), before)
    rank = jnp.sum(member * counts, axis=0, keepdims=True)
    g = jnp.where(moved, free + SLOTS * owner + rank, rank)

    mine = onehot(
        jnp.broadcast_to(g, (SLOTS, width))
        == sub_iota((SLOTS, width)) + (free + SLOTS * row).astype(F32)
    )
    spot = jnp.sum(mine * local_row, axis=1, keepdims=True)
    used = jnp.sum(mine, axis=1, keepdims=True)
    spot = jnp.where(used > 0.0, spot, -1.0)
    pick = onehot(jnp.broadcast_to(spot, (SLOTS, rows)) == lane_iota((SLOTS, rows))).astype(BF16)

    loads[2].wait()
    slots(z, core)[...] = select(pick, mat[...])

    @pl.when(is_root)
    def _():
        head = mat[0:width, :]
        unmoved = onehot(jnp.broadcast_to(g, (free, width)) == sub_iota((free, width))).astype(BF16)
        work[0:free, :] = select(unmoved, head)
        goal = jnp.where(moved, owner * SLOTS + rank, -1.0)
        total = n_row * SLOTS
        send_to = onehot(jnp.broadcast_to(goal, (total, width)) == sub_iota((total, width))).astype(BF16)
        init[...] = select(send_to, head)

    for t in range(NZ - 1):
        @pl.when(t < z)
        def _():
            own_slots(t).start()

    @pl.when(jnp.logical_not(first_core))
    def _():
        pass_slots(z).start()

    @pl.when(first_core)
    def _():
        pl.semaphore_wait(pready, 1)
        pass_slots(z).start()

    @pl.when(is_root)
    def _():
        u_pass().start()
        i_pass().start()
        for t in range(1, NZ // 2 + 1):
            root_serve(t)


    def permute_inverse():
        loads[3].wait()
        for ia, a in enumerate(ox):
            for ib, b in enumerate(oy):
                src = (lax.rem(x - s * a + 2 * NX, NX) * NY + lax.rem(y - s * b + 2 * NY, NY)) * 8
                dst = (ia * NY + ib) * 8
                inv_rel[dst:dst + 8, :] = inv[pl.ds(pl.multiple_of(src, 8), 8), :]
        parts = [g[:, i * 128:(i + 1) * 128] for i in range(width // 128)]
        while len(parts) < 8:
            parts = parts + parts
        flipped = jnp.concatenate(parts[:8], axis=0).T
        g_col = jnp.concatenate([flipped[:, i:i + 1] for i in range(width // 128)], axis=0)
        depth = work.shape[0]
        place_of = onehot(jnp.broadcast_to(g_col, (width, depth)) == lane_iota((width, depth))).astype(BF16)
        inv_hi, inv_lo = split2(inv_rel[...])
        lpe_hi[...] = dot(inv_hi, place_of).astype(BF16)
        lpe_lo[...] = dot(inv_lo, place_of).astype(BF16)

    def serve(q):
        t = z + q

        @pl.when((t < NZ) & jnp.logical_not(is_root))
        def _():
            pl.semaphore_wait(ready.at[t], 1)
            own_slots(t).start()

    def finish_upper():
        far_first = first_core & jnp.logical_not(source)

        @pl.when(far_first)
        def _():
            recv(u_rows, ur.at[0])
            u_pass().start()
            recv(i_pair(z), ifr.at[0])
            i_pass().start()

        def along_z(lo, hi):
            for t in range(lo, hi):
                @pl.when(z != t)
                def _():
                    recv(slots(t, core), zr.at[t])
                    pass_slots(t).start()

        def other_core(lo, hi):
            for t in range(lo, hi):
                recv(slots(t, 1 - core), zpr.at[t])

        along_z(0, NZ)

        @pl.when(jnp.logical_not(first_core))
        def _():
            recv(u_rows, upr.at[0])
            recv(i_rows(1), imr.at[0])

        other_core(0, NZ)

        v_hi, v_lo = split2(work[...])
        up[...] = dot(lpe_hi[...], v_hi) + dot(lpe_hi[...], v_lo) + dot(lpe_lo[...], v_hi)
        for ia in range(NX):
            for ib in range(NY):
                src, dst = (ia * NY + ib) * 8, (ib * NX + ia) * 8
                up_b[dst:dst + 8, :] = up[src:src + 8, :]

    leaves = []
    todo = [e for e in half_a.events() + half_b.events()]
    todo += [(1.5 + 1.05 * q, serve, q, 0) for q in range(1, NZ)]
    todo += [(1.5 * (t - NZ // 2 + 1), root_serve, t, 0) for t in range(NZ // 2 + 1, NZ)]
    todo.append((UPPER, finish_upper, 0, 0))
    todo.append((0.0, permute_inverse, 0, 0))
    for e in sorted(todo, key=lambda e: e[0]):
        _, what, o, k = e
        if what is serve:
            serve(o)
        elif what is root_serve:
            pl.when(is_root)(functools.partial(root_serve, o))
        elif what in (permute_inverse, finish_upper):
            what()
        elif o and not what.next_ones(o, what.n_out):
            leaves.append((what, o, k))
        else:
            what.arrive(o, k)

    parts = split2(i_rows(core)[...])
    ones = jnp.ones((SLOTS, 128), BF16)
    halves = []
    for n, (hf, u) in enumerate(((half_a, up), (half_b, up_b))):
        inner = sum(1 for o in hf.o_out if hf.next_ones(o, hf.n_out)) * hf.n_in * 8
        halves.append((slice(n * half, (n + 1) * half), hf, u, inner))

    def part(hf, u, k):
        p_hi, p_lo = split2(hf.buf[k, :])
        u_hi, u_lo = split2(u[k, :])
        return dot_t(p_hi, u_hi) + dot_t(p_hi, u_lo) + dot_t(p_lo, u_hi)

    for at, hf, u, inner in halves:
        place = pick[:, at]
        taken = dot_t(place, ones)
        taken = jnp.concatenate([taken] * (cols // 128), axis=1)
        new = dot_t(place, parts[0]) + dot_t(place, parts[1])
        mat[at, :] = jnp.where(taken > 0.5, new, mat[at, :]) - part(hf, u, slice(0, inner))

    for hf, o, k in leaves:
        hf.arrive(o, k)

    for at, hf, u, inner in halves:
        mat[at, :] = mat[at, :] - part(hf, u, slice(inner, width))

    @pl.when(is_root)
    def _():
        for ia, a in enumerate(ox):
            for ib, b in enumerate(oy):
                dst = (lax.rem(x - s * a + 2 * NX, NX) * NY + lax.rem(y - s * b + 2 * NY, NY)) * 8
                src = (ia * NY + ib) * 8
                mat[pl.ds(pl.multiple_of(dst, 8), 8), :] = up[src:src + 8, :]

    half_a.finish()
    half_b.finish()
    for t in range(NZ):
        @pl.when(z != t)
        def _():
            own_slots(t).wait_send()

        pass_slots(t).wait_send()

    @pl.when(is_root)
    def _():
        for t in range(1, NZ):
            u_copy(t).wait_send()
            i_copy(t).wait_send()

    @pl.when(first_core)
    def _():
        u_pass().wait_send()
        i_pass().wait_send()


def local(matrix, panel_t, inverse_lower, pivot_rows):
    rows, cols = matrix.shape
    width = inverse_lower.shape[0]
    depth = width // 2 + 2 * NZ * SLOTS
    half = panel_t.shape[1] // 2
    hbm, vmem = pl.BlockSpec(memory_space=pltpu.HBM), pl.BlockSpec(memory_space=pltpu.VMEM)
    dma, regular = pltpu.SemaphoreType.DMA, pltpu.SemaphoreType.REGULAR
    held = [pltpu.with_memory_space_constraint(v, pltpu.HBM) for v in (matrix, panel_t, inverse_lower)]
    return pl.pallas_call(
        kernel,
        out_shape=jax.ShapeDtypeStruct((rows, cols), F32),
        in_specs=[hbm, hbm, hbm, vmem],
        out_specs=vmem,
        scratch_shapes=[
            pltpu.VMEM((width, width), F32),
            pltpu.VMEM((width, width), F32),
            pltpu.VMEM((width, half), F32),
            pltpu.VMEM((width, half), F32),
            pltpu.VMEM((depth, cols), F32),
            pltpu.VMEM((2 * NZ * SLOTS, cols), F32),
            pltpu.VMEM((width, depth), BF16),
            pltpu.VMEM((width, depth), BF16),
            pltpu.VMEM((width, cols), F32),
            pltpu.VMEM((width, cols), F32),
            dma((4,)), dma((1,)), dma((1,)),
            dma((NY,)), dma((NX, len(groups_of(NY)))),
            dma((NX,)), dma((NY, len(groups_of(NX)))),
            dma((NZ,)), dma((NZ,)), dma((NZ,)), dma((NZ,)),
            dma((NZ,)), dma((1,)), dma((1,)), dma((1,)),
            dma((1,)), dma((1,)), dma((NZ,)), dma((1,)),
            regular((NZ,)), regular,
        ],
        compiler_params=pltpu.CompilerParams(
            collective_id=0, has_side_effects=True, vmem_limit_bytes=20 << 20
        ),
    )(*held, pivot_rows.reshape(1, width))


def solution(mesh):
    in_specs = (P("row", "col"), P("col", "row"), P(), P())
    out_specs = P("row", "col")
    return jax.shard_map(local, mesh=mesh, in_specs=in_specs, out_specs=out_specs, check_vma=False)
```
